32 devices in a mesh: groups: 2 (over x), sector: 16 (over z, y, core).
Axes of the slice: x: 2, y: 2, z: 4, core: 2. Of those that a mesh axis runs over, the one named last changes fastest.
Arguments:
- fields: bfloat16 [524288, 128], P(('groups', 'sector')), parts along dimension 0, may hold values from -6 to 6
- weights: bfloat16 [5120, 128, 128], P('sector'), may hold values from -0.25 to 0.25
- source_block: int32 [5120], P('sector'), may hold values from 0 to 127
- target_block: int32 [1280], P('sector'), may hold values from 0 to 1023, as said below
- area: float32 [131072], P('sector'), may hold values from 0.1 to 1
Outputs:
- level10: bfloat16 [262144, 128], P(('groups', 'sector')), parts along dimension 0
- level9: float32 [65536, 128], P(('groups', 'sector')), parts along dimension 0
- level8: float32 [16384, 128], P(('groups', 'sector')), parts along dimension 0
The draws below stay inside these ranges and needn't reach their ends.
There are 2 independent parts, one for each index of `groups`. The reference program is written for one: setup_inputs(seed, part) draws one part's arguments, and reference() takes and returns one part's arrays. A program takes and returns all parts, laid end to end along the dimension named above; an argument that names none is the same for every part. Nothing has to cross between parts.
Inputs may be any that keep to these rules, and one draw needn't show every extreme that they name: `target_block`: the partial blocks of one sector s (indices s * 80 to s * 80 + 79) name distinct target blocks; each target block b lies in sector b // 64, at most 2 sectors from s around the closed loop; at most 16 of them lie in any one sector other than s, and every sector has exactly 16 in one other sector.
All inputs are finite; a program needn't handle non-finite values.
Results may differ from the reference program's by a relative error of at most 0.0075.
Values may be sent and summed in bfloat16 or wider, within the bound.
A program may use at most 128 MiB of HBM per device.

```python
import math
import jax
import jax.numpy as jnp
from jax import lax

BLK = 128
PER_TGT = 4
REACH = 2
TB_DEV = 64
CAP = 16
NG_DEV = 80
SB_DEV = 128
NB_DEV = 320
COLS = 128
NPIX = 131072
NSRC = 262144
N_SECTOR = 16


def draw_target_block(key, part):
    width = 2 * REACH
    key_counts, key_forced, key_perms, key_order = jax.random.split(key, 4)
    others = jax.random.randint(key_counts, (N_SECTOR, width), 1, CAP + 1)
    forced = jax.random.randint(key_forced, (N_SECTOR,), 0, width)
    others = jnp.where(jnp.arange(width)[None, :] == forced[:, None], CAP, others)
    middle = NG_DEV - jnp.sum(others, axis=1)
    counts = jnp.concatenate([others[:, :REACH], middle[:, None], others[:, REACH:]], axis=1)
    ends = jnp.cumsum(counts, axis=1)
    starts = ends - counts
    slots = jnp.arange(NG_DEV)
    which = jnp.sum(slots[None, :, None] >= ends[:, None, :], axis=2)
    within = slots[None, :] - jnp.take_along_axis(starts, which, axis=1)
    perm_keys = jax.random.split(key_perms, N_SECTOR * (width + 1))
    perms = jax.vmap(lambda single: jax.random.permutation(single, TB_DEV))(perm_keys)
    perms = perms.reshape(N_SECTOR, width + 1, TB_DEV)
    chosen = perms[jnp.arange(N_SECTOR)[:, None], which, within]
    owners = (jnp.arange(N_SECTOR)[:, None] + which - REACH) % N_SECTOR
    blocks = owners * TB_DEV + chosen
    order_keys = jax.random.split(key_order, N_SECTOR)
    orders = jax.vmap(lambda single: jax.random.permutation(single, NG_DEV))(order_keys)
    blocks = jnp.take_along_axis(blocks, orders, axis=1)
    return blocks.reshape(-1).astype(jnp.int32)


def with_ends(array, own_key, least, high):
    longest = array.shape.index(max(array.shape))
    spots = []
    for shift in (0, 1):
        where = [jax.random.randint(jax.random.fold_in(own_key, axis), (), 0, length) for axis, length in enumerate(array.shape)]
        where[longest] = (where[longest] + shift) % array.shape[longest]
        spots.append(tuple(where))
    return array.at[spots[0]].set(least).at[spots[1]].set(high)


def block_levels(rng, extent, cuts, least, largest):
    level, own = 1.0, jax.random.fold_in(rng, 6)
    for dim, shards_of in cuts:
        steps = jnp.exp(jax.random.uniform(jax.random.fold_in(own, dim), (shards_of,), jnp.float32, least / len(cuts), largest / len(cuts)))
        level = level * jnp.repeat(steps, extent[dim] // shards_of).reshape([-1 if axis == dim else 1 for axis in range(len(extent))])
    return level


def gaussian(rng, shape, scale, limit, cuts=(), kind=jnp.bfloat16):
    entries = jax.random.normal(rng, shape, jnp.float32) * scale
    if len(cuts) > 0:
        entries = block_levels(rng, shape, cuts, -0.22, 0.18) * entries
    return jnp.clip(entries, min=-limit, max=limit).astype(kind)


def setup_inputs(seed: int = 0, part: int = 0) -> dict:
    seeds = jax.random.split(jax.random.key(seed), 6)
    part_keys = jax.random.split(jax.random.fold_in(seeds[5], part), 6)
    fields = gaussian(part_keys[0], (NSRC, COLS), 1.0, 6.0, ((0, 16),))
    weights = gaussian(seeds[1], (NB_DEV * N_SECTOR, BLK, BLK), (BLK * PER_TGT) ** -0.5, 0.25, ((0, 16),))
    source_block = with_ends(jax.random.randint(seeds[2], (NB_DEV * N_SECTOR,), 0, SB_DEV), jax.random.fold_in(seeds[2], 1), 0, SB_DEV - 1).astype(jnp.int32)
    target_block = draw_target_block(jax.random.fold_in(seeds[5], 71), part)
    area = jnp.clip(jnp.exp(math.log(1.0) - 2.3025851 * jax.random.uniform(seeds[4], (NPIX,), jnp.float32) ** block_levels(seeds[4], (NPIX,), ((0, 16),), -0.2, 0.2)), 0.1, 1.0)
    return dict(fields=fields, weights=weights, source_block=source_block, target_block=target_block, area=area)


def reference(fields, weights, source_block, target_block, area):
    cols = fields.shape[1]
    source_blocks = fields.reshape(-1, BLK, cols)
    weight_dev = weights.reshape(N_SECTOR, NB_DEV, BLK, BLK)
    source_dev = source_block.reshape(N_SECTOR, NB_DEV)
    target_dev = target_block.reshape(N_SECTOR, NG_DEV)
    sector_ids = jnp.arange(N_SECTOR).astype(jnp.int32)

    def one_sector(summed, items):
        wblocks, sources, targets, sector_id = items
        start = (sector_id * SB_DEV).astype(jnp.int32)
        own_blocks = lax.dynamic_slice_in_dim(source_blocks, start, SB_DEV, 0)
        picked = own_blocks[sources.astype(jnp.int32)]
        terms = jnp.einsum("kps,ksc->kpc", wblocks.astype(jnp.float32), picked.astype(jnp.float32))
        partial_value = terms.reshape(NG_DEV, PER_TGT, BLK, cols).sum(1).astype(jnp.bfloat16)
        summed = summed.at[targets.astype(jnp.int32)].add(partial_value.astype(jnp.float32))
        return summed, None

    start_sum = jnp.zeros((TB_DEV * N_SECTOR, BLK, cols), jnp.float32)
    summed, unused = lax.scan(one_sector, start_sum, (weight_dev, source_dev, target_dev, sector_ids))
    flat = summed.reshape(-1, cols)
    level10 = flat.astype(jnp.bfloat16)
    weighted = flat * area[:, None]
    level9 = weighted.reshape(-1, 4, cols).sum(1) / area.reshape(-1, 4).sum(1)[:, None]
    level8 = weighted.reshape(-1, 16, cols).sum(1) / area.reshape(-1, 16).sum(1)[:, None]
    return level10, level9, level8
```

```python
import functools

import jax
import jax.numpy as jnp
from jax import lax
from jax.experimental import pallas as pl
from jax.experimental.pallas import tpu as pltpu
from jax.sharding import PartitionSpec as P

CAP = 16
KINDS = 4
CHUNK = 4
STEP = 16
FIELD_PARTS = 4
WEIGHT_PARTS = 4
ANY = pl.BlockSpec(memory_space=pl.ANY)
HBM = pl.BlockSpec(memory_space=pltpu.HBM)
VMEM = pl.BlockSpec(memory_space=pltpu.VMEM)
MESH = pl.DeviceIdType.MESH


def offsets(me):
    even = lax.rem(me, 2) == 0
    return [2, -2, jnp.where(even, -1, 1), jnp.where(even, 1, -1)]


def tables(target, owned, firsts):
    groups = target.shape[0]
    row = target.reshape(1, groups)
    down = lax.broadcasted_iota(jnp.int32, (groups, groups), 0)
    across = lax.broadcasted_iota(jnp.int32, (groups, groups), 1)
    column = jnp.where(down == across, row, 0).sum(1, keepdims=True)

    def kinds_of(where_to):
        kind = jnp.full(where_to.shape, KINDS, jnp.int32)
        local = where_to - firsts[KINDS]
        for k in range(KINDS):
            inside = (where_to >= firsts[k]) & (where_to < firsts[k] + owned)
            kind = jnp.where(inside, k, kind)
            local = jnp.where(inside, where_to - firsts[k], local)
        return kind, local

    kind, local = kinds_of(column)
    before = (kind == kinds_of(row)[0]) & (across < down)
    rank = jnp.where(before, 1, 0).sum(1, keepdims=True)
    shape = (groups, 128)
    lane = lax.broadcasted_iota(jnp.int32, shape, 1)
    group = lax.broadcasted_iota(jnp.int32, shape, 0)
    chosen = jnp.where(kind * CAP + rank == lane, group, 0).max(0, keepdims=True)
    here = local == lane
    own = jnp.where(here & (kind == KINDS), group, groups).min(0, keepdims=True)
    slots = [
        jnp.where(here & (kind == k), jnp.minimum(rank, CAP), CAP).min(0, keepdims=True)
        for k in range(KINDS)
    ]
    return jnp.concatenate([chosen, own, *slots, chosen, chosen], axis=0)


def exchange_kernel(sectors, target_hbm, source_hbm, w_hbm, f_hbm, area_hbm, *rest):
    total, last, pool, slots_out = rest[:4]
    (target, mine, theirs, source, table, slots, area, wbuf, fbuf, sbuf), rest = rest[4:14], rest[14:]
    received, rest = list(rest[:3]), rest[3:]
    i_sem, t_sem, f_sem, w_sem, send_sem, recv_sem, tsend_sem, trecv_sem = rest
    received.insert(2, last)
    me = lax.axis_index("sector")
    owned, width, cols = total.shape
    groups = target.shape[0]
    nb = w_hbm.shape[0]
    per_group = nb // groups
    blocks = f_hbm.shape[0]
    places = [lax.rem(me + sectors + move, sectors) for move in offsets(me)]
    peers = [{"sector": place} for place in places]
    barrier = pltpu.get_barrier_semaphore()
    for peer in peers:
        pl.semaphore_signal(barrier, inc=1, device_id=peer, device_id_type=MESH)

    target_in = pltpu.make_async_copy(target_hbm, target, i_sem.at[0])
    source_in = pltpu.make_async_copy(source_hbm, source, i_sem.at[1])
    target_in.start()
    source_in.start()
    loads = [source_in]
    for ref, buf, sem, size in ((f_hbm, fbuf, f_sem, blocks), (w_hbm, wbuf, w_sem, nb)):
        parts = sem.shape[0]
        for i in range(parts):
            rows = pl.ds(i * (size // parts), size // parts)
            loads.append(pltpu.make_async_copy(ref.at[rows], buf.at[rows], sem.at[i]))
            loads[-1].start()
    area_in = pltpu.make_async_copy(area_hbm, area, i_sem.at[3])
    area_in.start()
    nothing = jnp.zeros((width, cols), jnp.bfloat16)
    fbuf[blocks] = nothing
    for k in range(KINDS):
        received[k][CAP] = nothing

    target_in.wait()
    firsts = [place * owned for place in places] + [me * owned]
    mine[...] = tables(target[...], owned, firsts)
    table_in = pltpu.make_async_copy(mine, table, i_sem.at[2])
    table_in.start()
    pl.semaphore_wait(barrier, KINDS)
    moved = []
    for k in range(KINDS):
        moved.append(
            pltpu.make_async_remote_copy(
                src_ref=mine,
                dst_ref=theirs.at[k],
                send_sem=tsend_sem.at[k],
                recv_sem=trecv_sem.at[k],
                device_id=peers[k],
                device_id_type=MESH,
            )
        )
        moved[-1].start()

    n9 = width // 4
    rows = pool.shape[1]
    row = lax.broadcasted_iota(jnp.int32, (rows, width), 0)
    pixel = lax.broadcasted_iota(jnp.int32, (rows, width), 1)
    member = jnp.where(row < n9, pixel // 4 - row, pixel // 16 - (row - n9)) == 0

    table_in.wait()
    for copy in loads:
        copy.wait()

    def product(g, absent=False):
        first = g * per_group
        left = jnp.concatenate([wbuf[first + q] for q in range(per_group)], axis=1)
        places = [jnp.where(absent, blocks, source[first + q]) for q in range(per_group)]
        right = jnp.concatenate([fbuf[place] for place in places], axis=0)
        return jnp.dot(left, right, preferred_element_type=jnp.float32)

    chunks = CAP // CHUNK

    def block_copy(k, c):
        return pltpu.make_async_remote_copy(
            src_ref=sbuf.at[pl.ds(k * CAP + c * CHUNK, CHUNK)],
            dst_ref=received[k].at[pl.ds(c * CHUNK, CHUNK)],
            send_sem=send_sem.at[k * chunks + c],
            recv_sem=recv_sem.at[k * chunks + c],
            device_id=peers[k],
            device_id_type=MESH,
        )

    for k in (0, 1, 3, 2):

        @pl.loop(0, chunks)
        def _(c):
            for r in range(CHUNK):
                slot = k * CAP + c * CHUNK + r
                sbuf[slot] = product(table[0, slot]).astype(jnp.bfloat16)
            block_copy(k, c).start()

    for copy in moved:
        copy.wait()
    slots_in = [pltpu.make_async_copy(theirs.at[k], slots.at[k], t_sem.at[k]) for k in range(KINDS)]
    slots_save = pltpu.make_async_copy(theirs.at[2], slots_out, t_sem.at[KINDS])
    for copy in (*slots_in, slots_save):
        copy.start()

    @pl.loop(0, owned // 2)
    def _(i):
        for j in range(2):
            g = table[1, 2 * i + j]
            total[2 * i + j] = product(jnp.minimum(g, groups - 1), g == groups)

    area_in.wait()

    @pl.loop(0, owned)
    def _(t):
        share = jnp.where(member, area[pl.ds(t, 1), :], 0.0)
        pool[t] = (share / share.sum(1, keepdims=True)).astype(pool.dtype)

    for copy in (*slots_in, slots_save):
        copy.wait()
    for k in (0, 1, 3):

        @pl.loop(0, chunks)
        def _(c):
            block_copy(k, c).wait()

    @pl.loop(0, owned // 2)
    def _(i):
        for j in range(2):
            t = 2 * i + j
            value = total[t]
            for k in (0, 1, 3):
                value = value + received[k][slots[k, 2 + k, t]].astype(jnp.float32)
            total[t] = value

    @pl.loop(0, chunks)
    def _(c):
        block_copy(2, c).wait()


def exchange(fields, weights, source_block, target_block, area, sectors):
    nb, width, _ = weights.shape
    cols = fields.shape[-1]
    groups = target_block.shape[0]
    owned = area.shape[0]
    blocks = fields.shape[0]
    block = (width, cols)
    chunks = CAP // CHUNK
    bf16, i32 = jnp.bfloat16, jnp.int32
    operands = (target_block, source_block, weights, fields, area)
    return pl.pallas_call(
        functools.partial(exchange_kernel, sectors),
        out_shape=[
            jax.ShapeDtypeStruct((owned, *block), jnp.float32),
            jax.ShapeDtypeStruct((CAP + 1, *block), bf16),
            jax.ShapeDtypeStruct((owned, width // 4 + width // 16, width), bf16),
            jax.ShapeDtypeStruct((8, 128), i32),
        ],
        in_specs=[HBM] * 5,
        out_specs=[VMEM] * 3 + [HBM],
        scratch_shapes=[
            pltpu.VMEM((groups,), i32),
            pltpu.VMEM((8, 128), i32),
            pltpu.VMEM((KINDS, 8, 128), i32),
            pltpu.SMEM((nb,), i32),
            pltpu.SMEM((8, 128), i32),
            pltpu.SMEM((KINDS, 8, 128), i32),
            pltpu.VMEM(area.shape, jnp.float32),
            pltpu.VMEM(weights.shape, bf16),
            pltpu.VMEM((blocks + 1, *block), bf16),
            pltpu.VMEM((KINDS * CAP, *block), bf16),
        ]
        + [pltpu.VMEM((CAP + 1, *block), bf16)] * 3
        + [
            pltpu.SemaphoreType.DMA((4,)),
            pltpu.SemaphoreType.DMA((KINDS + 1,)),
            pltpu.SemaphoreType.DMA((FIELD_PARTS,)),
            pltpu.SemaphoreType.DMA((WEIGHT_PARTS,)),
            pltpu.SemaphoreType.DMA((KINDS * chunks,)),
            pltpu.SemaphoreType.DMA((KINDS * chunks,)),
            pltpu.SemaphoreType.DMA((KINDS,)),
            pltpu.SemaphoreType.DMA((KINDS,)),
        ],
        compiler_params=pltpu.CompilerParams(
            collective_id=0, has_side_effects=True, vmem_limit_bytes=32 * 2**20
        ),
        name="exchange",
    )(*(pltpu.with_memory_space_constraint(x, pltpu.HBM) for x in operands))


def finish_kernel(total, last, pool, slots_hbm, *rest):
    outs_hbm, outs, slots, in_sem, out_sem = rest[:3], rest[3:6], *rest[6:]
    ten, nine, eight = outs
    owned = total.shape[0]
    n9 = nine.shape[1]
    copy = pltpu.make_async_copy(slots_hbm, slots, in_sem)
    copy.start()
    copy.wait()

    def results(c):
        rows = pl.ds(c * STEP, STEP)
        return [
            pltpu.make_async_copy(outs[i].at[rows], outs_hbm[i].at[rows], out_sem.at[3 * c + i])
            for i in range(3)
        ]

    @pl.loop(0, owned // STEP)
    def _(c):
        for j in range(STEP):
            t = c * STEP + j
            value = total[t] + last[slots[4, t]].astype(jnp.float32)
            rounded = value.astype(jnp.bfloat16)
            ten[t] = rounded
            means = jnp.dot(pool[t], rounded, preferred_element_type=jnp.float32)
            nine[t] = means[:n9]
            eight[t] = means[n9:]
        for copy in results(c):
            copy.start()

    @pl.loop(0, owned // STEP)
    def _(c):
        for copy in results(c):
            copy.wait()


def finish(total, last, pool, slots):
    owned, width, cols = total.shape
    outs = [
        jax.ShapeDtypeStruct((owned, width, cols), jnp.bfloat16),
        jax.ShapeDtypeStruct((owned, width // 4, cols), jnp.float32),
        jax.ShapeDtypeStruct((owned, width // 16, cols), jnp.float32),
    ]
    return pl.pallas_call(
        finish_kernel,
        out_shape=outs,
        in_specs=[VMEM] * 3 + [HBM],
        out_specs=[HBM] * 3,
        scratch_shapes=[pltpu.VMEM(out.shape, out.dtype) for out in outs]
        + [
            pltpu.SMEM(slots.shape, jnp.int32),
            pltpu.SemaphoreType.DMA,
            pltpu.SemaphoreType.DMA((3 * (owned // STEP),)),
        ],
        compiler_params=pltpu.CompilerParams(vmem_limit_bytes=16 * 2**20),
        name="finish",
    )(total, last, pool, slots)


def per_device(fields, weights, source_block, target_block, area):
    width = weights.shape[1]
    cols = fields.shape[1]
    owned = area.shape[0] // width
    sectors = lax.axis_size("sector")
    blocks = fields.reshape(-1, width, cols)
    parts = exchange(
        blocks, weights, source_block, target_block, area.reshape(owned, width), sectors
    )
    ten, nine, eight = finish(*parts)
    return ten.reshape(-1, cols), nine.reshape(-1, cols), eight.reshape(-1, cols)


def solution(mesh):
    in_specs = (
        P(("groups", "sector"), None),
        P("sector", None, None),
        P("sector"),
        P("sector"),
        P("sector"),
    )
    out_specs = (P(("groups", "sector"), None),) * 3
    return jax.shard_map(
        per_device, mesh=mesh, in_specs=in_specs, out_specs=out_specs, check_vma=False
    )
```

```python
import functools

import jax
import jax.numpy as jnp
from jax import lax
from jax.experimental import pallas as pl
from jax.experimental.pallas import tpu as pltpu
from jax.sharding import PartitionSpec as P

CAP = 16
KINDS = 4
SCHEDULE = ((0, 0, 4), (0, 4, 12), (1, 0, 16), (3, 0, 16), (2, 0, 16))
UNROLL = 4
EARLY = (0, 1, 3)
LATE = (2,)
SLOTS = CAP + 1
STEP = 16
FIELD_PARTS = 2
WEIGHT_PARTS = 4
ANY = pl.BlockSpec(memory_space=pl.ANY)
HBM = pl.BlockSpec(memory_space=pltpu.HBM)
VMEM = pl.BlockSpec(memory_space=pltpu.VMEM)
MESH = pl.DeviceIdType.MESH


def offsets(me):
    near = jnp.where(lax.rem(me // 2, 2) == 0, 2, -2)
    here = jnp.where(lax.rem(me, 2) == 0, 1, -1)
    return [near, -near, -here, here]


def tables(target, owned, firsts):
    groups = target.shape[0]
    row = target.reshape(1, groups)
    down = lax.broadcasted_iota(jnp.int32, (groups, groups), 0)
    across = lax.broadcasted_iota(jnp.int32, (groups, groups), 1)
    column = jnp.where(down == across, row, 0).sum(1, keepdims=True)

    def kinds_of(where_to):
        kind = jnp.full(where_to.shape, KINDS, jnp.int32)
        local = where_to - firsts[KINDS]
        for k in range(KINDS):
            inside = (where_to >= firsts[k]) & (where_to < firsts[k] + owned)
            kind = jnp.where(inside, k, kind)
            local = jnp.where(inside, where_to - firsts[k], local)
        return kind, local

    kind, local = kinds_of(column)
    before = (kind == kinds_of(row)[0]) & (across < down)
    rank = jnp.where(before, 1, 0).sum(1, keepdims=True)
    shape = (groups, 128)
    lane = lax.broadcasted_iota(jnp.int32, shape, 1)
    group = lax.broadcasted_iota(jnp.int32, shape, 0)
    chosen = jnp.where(kind * CAP + rank == lane, group, 0).max(0, keepdims=True)
    here = local == lane
    own = jnp.where(here & (kind == KINDS), group, groups).min(0, keepdims=True)
    slots = [
        jnp.where(here & (kind == k), jnp.minimum(rank, CAP), CAP).min(0, keepdims=True)
        for k in range(KINDS)
    ]
    return jnp.concatenate([chosen, own, *slots, chosen, chosen], axis=0)


def turned(row, length):
    shape = (length, row.shape[1])
    down = lax.broadcasted_iota(jnp.int32, shape, 0)
    across = lax.broadcasted_iota(jnp.int32, shape, 1)
    column = jnp.where(down == across, row, 0).sum(1, keepdims=True)
    return jnp.broadcast_to(column, shape)


def exchange_kernel(sectors, target_hbm, source_hbm, w_hbm, f_hbm, area_hbm, *rest):
    total, received_late, pool, late = rest[:4]
    (target, mine, theirs, source, table, slots, area, wbuf, fbuf, sbuf, received), rest = rest[4:15], rest[15:]
    i_sem, t_sem, f_sem, w_sem, send_sem, recv_sem, tsend_sem, trecv_sem = rest
    me = lax.axis_index("sector")
    owned, width, cols = total.shape
    groups = target.shape[0]
    nb = w_hbm.shape[0]
    per_group = nb // groups
    blocks = f_hbm.shape[0]
    places = [lax.rem(me + sectors + move, sectors) for move in offsets(me)]
    peers = [{"sector": place} for place in places]
    barrier = pltpu.get_barrier_semaphore()
    for peer in peers:
        pl.semaphore_signal(barrier, inc=1, device_id=peer, device_id_type=MESH)

    target_in = pltpu.make_async_copy(target_hbm, target, i_sem.at[0])
    source_in = pltpu.make_async_copy(source_hbm, source, i_sem.at[1])
    target_in.start()
    source_in.start()
    loads = [source_in]
    for ref, buf, sem, size in ((f_hbm, fbuf, f_sem, blocks), (w_hbm, wbuf, w_sem, nb)):
        parts = sem.shape[0]
        for i in range(parts):
            rows = pl.ds(i * (size // parts), size // parts)
            loads.append(pltpu.make_async_copy(ref.at[rows], buf.at[rows], sem.at[i]))
            loads[-1].start()
    area_in = pltpu.make_async_copy(area_hbm, area, i_sem.at[3])
    area_in.start()
    nothing = jnp.zeros((width, cols), jnp.bfloat16)
    fbuf[blocks] = nothing
    for k in range(len(EARLY)):
        received[k * SLOTS + CAP] = nothing
    for k in range(len(LATE)):
        received_late[k * SLOTS + CAP] = nothing

    target_in.wait()
    firsts = [place * owned for place in places] + [me * owned]
    mine[...] = tables(target[...], owned, firsts)
    table_in = pltpu.make_async_copy(mine, table, i_sem.at[2])
    table_in.start()
    pl.semaphore_wait(barrier, KINDS)
    moved = []
    for k in range(KINDS):
        moved.append(
            pltpu.make_async_remote_copy(
                src_ref=mine,
                dst_ref=theirs.at[k],
                send_sem=tsend_sem.at[k],
                recv_sem=trecv_sem.at[k],
                device_id=peers[k],
                device_id_type=MESH,
            )
        )
        moved[-1].start()

    n9 = width // 4
    rows = pool.shape[1]
    row = lax.broadcasted_iota(jnp.int32, (rows, width), 0)
    pixel = lax.broadcasted_iota(jnp.int32, (rows, width), 1)
    member = jnp.where(row < n9, pixel // 4 - row, pixel // 16 - (row - n9)) == 0

    table_in.wait()
    for copy in loads:
        copy.wait()

    def product(g, absent=False):
        first = g * per_group
        left = jnp.concatenate([wbuf[first + q] for q in range(per_group)], axis=1)
        places = [jnp.where(absent, blocks, source[first + q]) for q in range(per_group)]
        right = jnp.concatenate([fbuf[place] for place in places], axis=0)
        return jnp.dot(left, right, preferred_element_type=jnp.float32)

    messages = []
    for i, (k, first, count) in enumerate(SCHEDULE):
        landing = received if k in EARLY else received_late
        start = (EARLY if k in EARLY else LATE).index(k) * SLOTS

        @pl.loop(0, count // UNROLL)
        def _(c):
            for r in range(UNROLL):
                slot = k * CAP + first + c * UNROLL + r
                sbuf[slot] = product(table[0, slot]).astype(jnp.bfloat16)

        message = pltpu.make_async_remote_copy(
            src_ref=sbuf.at[pl.ds(k * CAP + first, count)],
            dst_ref=landing.at[pl.ds(start + first, count)],
            send_sem=send_sem.at[i],
            recv_sem=recv_sem.at[i],
            device_id=peers[k],
            device_id_type=MESH,
        )
        message.start()
        messages.append((k, message))

    for copy in moved:
        copy.wait()
    slots_in = [pltpu.make_async_copy(theirs.at[k], slots.at[k], t_sem.at[k]) for k in range(KINDS)]
    for copy in slots_in:
        copy.start()
    for i, k in enumerate(LATE):
        late[i] = turned(theirs[k, 2 + k : 3 + k, :], owned)

    @pl.loop(0, owned // 2)
    def _(i):
        for j in range(2):
            g = table[1, 2 * i + j]
            total[2 * i + j] = product(jnp.minimum(g, groups - 1), g == groups)

    area_in.wait()

    @pl.loop(0, owned)
    def _(t):
        share = jnp.where(member, area[pl.ds(t, 1), :], 0.0)
        pool[t] = (share / share.sum(1, keepdims=True)).astype(pool.dtype)

    for copy in slots_in:
        copy.wait()
    for k, message in messages:
        if k in EARLY:
            message.wait()

    @pl.loop(0, owned // 2)
    def _(i):
        for j in range(2):
            t = 2 * i + j
            value = total[t]
            for e, k in enumerate(EARLY):
                value = value + received[e * SLOTS + slots[k, 2 + k, t]].astype(jnp.float32)
            total[t] = value

    for k, message in messages:
        if k in LATE:
            message.wait()


def exchange(fields, weights, source_block, target_block, area, sectors):
    nb, width, _ = weights.shape
    cols = fields.shape[-1]
    groups = target_block.shape[0]
    owned = area.shape[0]
    blocks = fields.shape[0]
    block = (width, cols)
    bf16, i32 = jnp.bfloat16, jnp.int32
    operands = (target_block, source_block, weights, fields, area)
    return pl.pallas_call(
        functools.partial(exchange_kernel, sectors),
        out_shape=[
            jax.ShapeDtypeStruct((owned, *block), jnp.float32),
            jax.ShapeDtypeStruct((len(LATE) * SLOTS, *block), bf16),
            jax.ShapeDtypeStruct((owned, width // 4 + width // 16, width), bf16),
            jax.ShapeDtypeStruct((len(LATE), owned, 128), i32),
        ],
        in_specs=[HBM] * 5,
        out_specs=[VMEM] * 4,
        scratch_shapes=[
            pltpu.VMEM((groups,), i32),
            pltpu.VMEM((8, 128), i32),
            pltpu.VMEM((KINDS, 8, 128), i32),
            pltpu.SMEM((nb,), i32),
            pltpu.SMEM((8, 128), i32),
            pltpu.SMEM((KINDS, 8, 128), i32),
            pltpu.VMEM(area.shape, jnp.float32),
            pltpu.VMEM(weights.shape, bf16),
            pltpu.VMEM((blocks + 1, *block), bf16),
            pltpu.VMEM((KINDS * CAP, *block), bf16),
            pltpu.VMEM((len(EARLY) * SLOTS, *block), bf16),
        ]
        + [
            pltpu.SemaphoreType.DMA((4,)),
            pltpu.SemaphoreType.DMA((KINDS,)),
            pltpu.SemaphoreType.DMA((FIELD_PARTS,)),
            pltpu.SemaphoreType.DMA((WEIGHT_PARTS,)),
            pltpu.SemaphoreType.DMA((len(SCHEDULE),)),
            pltpu.SemaphoreType.DMA((len(SCHEDULE),)),
            pltpu.SemaphoreType.DMA((KINDS,)),
            pltpu.SemaphoreType.DMA((KINDS,)),
        ],
        compiler_params=pltpu.CompilerParams(
            collective_id=0, has_side_effects=True, vmem_limit_bytes=32 * 2**20
        ),
        name="exchange",
    )(*(pltpu.with_memory_space_constraint(x, pltpu.HBM) for x in operands))


def finish_kernel(total, received, pool, late, *rest):
    outs_hbm, outs, out_sem = rest[:3], rest[3:6], rest[6]
    ten, nine, eight = outs
    owned = total.shape[0]
    n9 = nine.shape[1]

    def results(c):
        rows = pl.ds(c * STEP, STEP)
        return [
            pltpu.make_async_copy(outs[i].at[rows], outs_hbm[i].at[rows], out_sem.at[3 * c + i])
            for i in range(3)
        ]

    @pl.loop(0, owned // STEP)
    def _(c):
        places = [late[i, pl.ds(c * STEP, STEP), :] for i in range(len(LATE))]
        for j in range(STEP):
            t = c * STEP + j
            value = total[t]
            for i in range(len(LATE)):
                value = value + received[i * SLOTS + places[i][j, 0]].astype(jnp.float32)
            rounded = value.astype(jnp.bfloat16)
            ten[t] = rounded
            means = jnp.dot(pool[t], rounded, preferred_element_type=jnp.float32)
            nine[t] = means[:n9]
            eight[t] = means[n9:]
        for copy in results(c):
            copy.start()

    @pl.loop(0, owned // STEP)
    def _(c):
        for copy in results(c):
            copy.wait()


def finish(total, received, pool, late):
    owned, width, cols = total.shape
    outs = [
        jax.ShapeDtypeStruct((owned, width, cols), jnp.bfloat16),
        jax.ShapeDtypeStruct((owned, width // 4, cols), jnp.float32),
        jax.ShapeDtypeStruct((owned, width // 16, cols), jnp.float32),
    ]
    return pl.pallas_call(
        finish_kernel,
        out_shape=outs,
        in_specs=[VMEM] * 4,
        out_specs=[HBM] * 3,
        scratch_shapes=[pltpu.VMEM(out.shape, out.dtype) for out in outs]
        + [
            pltpu.SemaphoreType.DMA((3 * (owned // STEP),)),
        ],
        compiler_params=pltpu.CompilerParams(vmem_limit_bytes=16 * 2**20),
        name="finish",
    )(total, received, pool, late)


def per_device(fields, weights, source_block, target_block, area):
    width = weights.shape[1]
    cols = fields.shape[1]
    owned = area.shape[0] // width
    sectors = lax.axis_size("sector")
    blocks = fields.reshape(-1, width, cols)
    parts = exchange(
        blocks, weights, source_block, target_block, area.reshape(owned, width), sectors
    )
    ten, nine, eight = finish(*parts)
    return ten.reshape(-1, cols), nine.reshape(-1, cols), eight.reshape(-1, cols)


def solution(mesh):
    in_specs = (
        P(("groups", "sector"), None),
        P("sector", None, None),
        P("sector"),
        P("sector"),
        P("sector"),
    )
    out_specs = (P(("groups", "sector"), None),) * 3
    return jax.shard_map(
        per_device, mesh=mesh, in_specs=in_specs, out_specs=out_specs, check_vma=False
    )
```

```python
import functools

import jax
import jax.numpy as jnp
from jax import lax
from jax.experimental import pallas as pl
from jax.experimental.pallas import tpu as pltpu
from jax.sharding import PartitionSpec as P

CAP = 16
KINDS = 4
SCHEDULE = ((0, 0, 4), (0, 4, 12), (1, 0, 16), (3, 0, 16), (2, 0, 16))
UNROLL = 4
EARLY = (0, 1, 3)
LATE = (2,)
SLOTS = CAP + 1
STEP = 16
FIELD_PARTS = 2
WEIGHT_PARTS = 4
ANY = pl.BlockSpec(memory_space=pl.ANY)
HBM = pl.BlockSpec(memory_space=pltpu.HBM)
VMEM = pl.BlockSpec(memory_space=pltpu.VMEM)
MESH = pl.DeviceIdType.MESH


def offsets(me):
    near = jnp.where(lax.rem(me // 2, 2) == 0, 2, -2)
    here = jnp.where(lax.rem(me, 2) == 0, 1, -1)
    return [near, -near, -here, here]


def tables(target, owned, firsts):
    groups = target.shape[0]
    row = target.reshape(1, groups)
    down = lax.broadcasted_iota(jnp.int32, (groups, groups), 0)
    across = lax.broadcasted_iota(jnp.int32, (groups, groups), 1)
    column = jnp.where(down == across, row, 0).sum(1, keepdims=True)

    def kinds_of(where_to):
        kind = jnp.full(where_to.shape, KINDS, jnp.int32)
        local = where_to - firsts[KINDS]
        for k in range(KINDS):
            inside = (where_to >= firsts[k]) & (where_to < firsts[k] + owned)
            kind = jnp.where(inside, k, kind)
            local = jnp.where(inside, where_to - firsts[k], local)
        return kind, local

    kind, local = kinds_of(column)
    before = (kind == kinds_of(row)[0]) & (across < down)
    rank = jnp.where(before, 1, 0).sum(1, keepdims=True)
    shape = (groups, 128)
    lane = lax.broadcasted_iota(jnp.int32, shape, 1)
    group = lax.broadcasted_iota(jnp.int32, shape, 0)
    chosen = jnp.where(kind * CAP + rank == lane, group, 0).max(0, keepdims=True)
    here = local == lane
    own = jnp.where(here & (kind == KINDS), group, groups).min(0, keepdims=True)
    slots = [
        jnp.where(here & (kind == k), jnp.minimum(rank, CAP), CAP).min(0, keepdims=True)
        for k in range(KINDS)
    ]
    return jnp.concatenate([chosen, own, *slots, chosen, chosen], axis=0)


def turned(row, length):
    shape = (length, row.shape[1])
    down = lax.broadcasted_iota(jnp.int32, shape, 0)
    across = lax.broadcasted_iota(jnp.int32, shape, 1)
    column = jnp.where(down == across, row, 0).sum(1, keepdims=True)
    return jnp.broadcast_to(column, shape)


def exchange_kernel(sectors, target_hbm, source_hbm, w_hbm, f_hbm, area_hbm, *rest):
    total, received_late, pool, late = rest[:4]
    (target, mine, theirs, source, table, slots, area, wbuf, fbuf, sbuf, received), rest = rest[4:15], rest[15:]
    i_sem, t_sem, f_sem, w_sem, send_sem, recv_sem, tsend_sem, trecv_sem = rest
    me = lax.axis_index("sector")
    owned, width, cols = total.shape
    groups = target.shape[0]
    nb = w_hbm.shape[0]
    per_group = nb // groups
    blocks = f_hbm.shape[0]
    places = [lax.rem(me + sectors + move, sectors) for move in offsets(me)]
    peers = [{"sector": place} for place in places]
    barrier = pltpu.get_barrier_semaphore()
    for peer in peers:
        pl.semaphore_signal(barrier, inc=1, device_id=peer, device_id_type=MESH)

    target_in = pltpu.make_async_copy(target_hbm, target, i_sem.at[0])
    source_in = pltpu.make_async_copy(source_hbm, source, i_sem.at[1])
    target_in.start()
    source_in.start()
    loads = [source_in]
    for ref, buf, sem, size in ((f_hbm, fbuf, f_sem, blocks), (w_hbm, wbuf, w_sem, nb)):
        parts = sem.shape[0]
        for i in range(parts):
            rows = pl.ds(i * (size // parts), size // parts)
            loads.append(pltpu.make_async_copy(ref.at[rows], buf.at[rows], sem.at[i]))
            loads[-1].start()
    area_in = pltpu.make_async_copy(area_hbm, area, i_sem.at[3])
    area_in.start()
    nothing = jnp.zeros((width, cols), jnp.bfloat16)
    fbuf[blocks] = nothing
    for k in range(len(EARLY)):
        received[k * SLOTS + CAP] = nothing
    for k in range(len(LATE)):
        received_late[k * SLOTS + CAP] = nothing

    target_in.wait()
    firsts = [place * owned for place in places] + [me * owned]
    mine[...] = tables(target[...], owned, firsts)
    table_in = pltpu.make_async_copy(mine, table, i_sem.at[2])
    table_in.start()
    pl.semaphore_wait(barrier, KINDS)
    moved = []
    for k in range(KINDS):
        moved.append(
            pltpu.make_async_remote_copy(
                src_ref=mine,
                dst_ref=theirs.at[k],
                send_sem=tsend_sem.at[k],
                recv_sem=trecv_sem.at[k],
                device_id=peers[k],
                device_id_type=MESH,
            )
        )
        moved[-1].start()

    n9 = width // 4
    rows = pool.shape[1]
    row = lax.broadcasted_iota(jnp.int32, (rows, width), 0)
    pixel = lax.broadcasted_iota(jnp.int32, (rows, width), 1)
    member = jnp.where(row < n9, pixel // 4 - row, pixel // 16 - (row - n9)) == 0

    table_in.wait()
    for copy in loads:
        copy.wait()

    def product(g, absent=False):
        first = g * per_group
        left = jnp.concatenate([wbuf[first + q] for q in range(per_group)], axis=1)
        places = [jnp.where(absent, blocks, source[first + q]) for q in range(per_group)]
        right = jnp.concatenate([fbuf[place] for place in places], axis=0)
        return jnp.dot(left, right, preferred_element_type=jnp.float32)

    messages = []
    for i, (k, first, count) in enumerate(SCHEDULE):
        landing = received if k in EARLY else received_late
        start = (EARLY if k in EARLY else LATE).index(k) * SLOTS

        @pl.loop(0, count // UNROLL)
        def _(c):
            for r in range(UNROLL):
                slot = k * CAP + first + c * UNROLL + r
                sbuf[slot] = product(table[0, slot]).astype(jnp.bfloat16)

        message = pltpu.make_async_remote_copy(
            src_ref=sbuf.at[pl.ds(k * CAP + first, count)],
            dst_ref=landing.at[pl.ds(start + first, count)],
            send_sem=send_sem.at[i],
            recv_sem=recv_sem.at[i],
            device_id=peers[k],
            device_id_type=MESH,
        )
        message.start()
        messages.append((k, message))

    for copy in moved:
        copy.wait()
    slots_in = [pltpu.make_async_copy(theirs.at[k], slots.at[k], t_sem.at[k]) for k in range(KINDS)]
    for copy in slots_in:
        copy.start()
    for i, k in enumerate(LATE):
        late[i] = turned(theirs[k, 2 + k : 3 + k, :], owned)

    @pl.loop(0, owned // 2)
    def _(i):
        for j in range(2):
            g = table[1, 2 * i + j]
            total[2 * i + j] = product(jnp.minimum(g, groups - 1), g == groups)

    area_in.wait()

    @pl.loop(0, owned)
    def _(t):
        share = jnp.where(member, area[pl.ds(t, 1), :], 0.0)
        pool[t] = (share / share.sum(1, keepdims=True)).astype(pool.dtype)

    for copy in slots_in:
        copy.wait()
    for k, message in messages:
        if k in EARLY:
            message.wait()

    @pl.loop(0, owned // 2)
    def _(i):
        for j in range(2):
            t = 2 * i + j
            value = total[t]
            for e, k in enumerate(EARLY):
                value = value + received[e * SLOTS + slots[k, 2 + k, t]].astype(jnp.float32)
            total[t] = value

    for k, message in messages:
        if k in LATE:
            message.wait()


def exchange(fields, weights, source_block, target_block, area, sectors):
    nb, width, _ = weights.shape
    cols = fields.shape[-1]
    groups = target_block.shape[0]
    owned = area.shape[0]
    blocks = fields.shape[0]
    block = (width, cols)
    bf16, i32 = jnp.bfloat16, jnp.int32
    operands = (target_block, source_block, weights, fields, area)
    return pl.pallas_call(
        functools.partial(exchange_kernel, sectors),
        out_shape=[
            jax.ShapeDtypeStruct((owned, *block), jnp.float32),
            jax.ShapeDtypeStruct((len(LATE) * SLOTS, *block), bf16),
            jax.ShapeDtypeStruct((owned, width // 4 + width // 16, width), bf16),
            jax.ShapeDtypeStruct((len(LATE), owned, 128), i32),
        ],
        in_specs=[HBM] * 5,
        out_specs=[VMEM] * 4,
        scratch_shapes=[
            pltpu.VMEM((groups,), i32),
            pltpu.VMEM((8, 128), i32),
            pltpu.VMEM((KINDS, 8, 128), i32),
            pltpu.SMEM((nb,), i32),
            pltpu.SMEM((8, 128), i32),
            pltpu.SMEM((KINDS, 8, 128), i32),
            pltpu.VMEM(area.shape, jnp.float32),
            pltpu.VMEM(weights.shape, bf16),
            pltpu.VMEM((blocks + 1, *block), bf16),
            pltpu.VMEM((KINDS * CAP, *block), bf16),
            pltpu.VMEM((len(EARLY) * SLOTS, *block), bf16),
        ]
        + [
            pltpu.SemaphoreType.DMA((4,)),
            pltpu.SemaphoreType.DMA((KINDS,)),
            pltpu.SemaphoreType.DMA((FIELD_PARTS,)),
            pltpu.SemaphoreType.DMA((WEIGHT_PARTS,)),
            pltpu.SemaphoreType.DMA((len(SCHEDULE),)),
            pltpu.SemaphoreType.DMA((len(SCHEDULE),)),
            pltpu.SemaphoreType.DMA((KINDS,)),
            pltpu.SemaphoreType.DMA((KINDS,)),
        ],
        compiler_params=pltpu.CompilerParams(
            collective_id=0, has_side_effects=True, vmem_limit_bytes=32 * 2**20
        ),
        name="exchange",
    )(*(pltpu.with_memory_space_constraint(x, pltpu.HBM) for x in operands))


def finish_kernel(total, received, pool, late, *rest):
    outs_hbm, outs, out_sem = rest[:3], rest[3:6], rest[6]
    ten, nine, eight = outs
    owned = total.shape[0]
    n9 = nine.shape[1]

    def results(c):
        rows = pl.ds(c * STEP, STEP)
        return [
            pltpu.make_async_copy(outs[i].at[rows], outs_hbm[i].at[rows], out_sem.at[3 * c + i])
            for i in range(3)
        ]

    for c in range(owned // STEP):
        places = [late[i, pl.ds(c * STEP, STEP), :] for i in range(len(LATE))]
        for j in range(STEP):
            t = c * STEP + j
            value = total[t]
            for i in range(len(LATE)):
                value = value + received[i * SLOTS + places[i][j, 0]].astype(jnp.float32)
            rounded = value.astype(jnp.bfloat16)
            ten[t] = rounded
            means = jnp.dot(pool[t], rounded, preferred_element_type=jnp.float32)
            nine[t] = means[:n9]
            eight[t] = means[n9:]
        for copy in results(c):
            copy.start()

    @pl.loop(0, owned // STEP)
    def _(c):
        for copy in results(c):
            copy.wait()


def finish(total, received, pool, late):
    owned, width, cols = total.shape
    outs = [
        jax.ShapeDtypeStruct((owned, width, cols), jnp.bfloat16),
        jax.ShapeDtypeStruct((owned, width // 4, cols), jnp.float32),
        jax.ShapeDtypeStruct((owned, width // 16, cols), jnp.float32),
    ]
    return pl.pallas_call(
        finish_kernel,
        out_shape=outs,
        in_specs=[VMEM] * 4,
        out_specs=[HBM] * 3,
        scratch_shapes=[pltpu.VMEM(out.shape, out.dtype) for out in outs]
        + [
            pltpu.SemaphoreType.DMA((3 * (owned // STEP),)),
        ],
        compiler_params=pltpu.CompilerParams(vmem_limit_bytes=16 * 2**20),
        name="finish",
    )(total, received, pool, late)


def per_device(fields, weights, source_block, target_block, area):
    width = weights.shape[1]
    cols = fields.shape[1]
    owned = area.shape[0] // width
    sectors = lax.axis_size("sector")
    blocks = fields.reshape(-1, width, cols)
    parts = exchange(
        blocks, weights, source_block, target_block, area.reshape(owned, width), sectors
    )
    ten, nine, eight = finish(*parts)
    return ten.reshape(-1, cols), nine.reshape(-1, cols), eight.reshape(-1, cols)


def solution(mesh):
    in_specs = (
        P(("groups", "sector"), None),
        P("sector", None, None),
        P("sector"),
        P("sector"),
        P("sector"),
    )
    out_specs = (P(("groups", "sector"), None),) * 3
    return jax.shard_map(
        per_device, mesh=mesh, in_specs=in_specs, out_specs=out_specs, check_vma=False
    )
```

```python
import functools

import jax
import jax.numpy as jnp
from jax import lax
from jax.experimental import pallas as pl
from jax.experimental.pallas import tpu as pltpu
from jax.sharding import PartitionSpec as P

CAP = 16
KINDS = 4
SCHEDULE = ((0, 0, 4), (0, 4, 12), (1, 0, 16), (3, 0, 16), (2, 0, 16))
UNROLL = 4
EARLY = (0, 1, 3)
LATE = (2,)
SLOTS = CAP + 1
STEP = 16
FIELD_PARTS = 2
WEIGHT_PARTS = 4
ANY = pl.BlockSpec(memory_space=pl.ANY)
HBM = pl.BlockSpec(memory_space=pltpu.HBM)
VMEM = pl.BlockSpec(memory_space=pltpu.VMEM)
MESH = pl.DeviceIdType.MESH


def offsets(me):
    near = jnp.where(lax.rem(me // 2, 2) == 0, 2, -2)
    here = jnp.where(lax.rem(me, 2) == 0, 1, -1)
    return [near, -near, -here, here]


def tables(target, owned, firsts):
    groups = target.shape[0]
    row = target.reshape(1, groups)
    down = lax.broadcasted_iota(jnp.int32, (groups, groups), 0)
    across = lax.broadcasted_iota(jnp.int32, (groups, groups), 1)
    column = jnp.where(down == across, row, 0).sum(1, keepdims=True)

    def kinds_of(where_to):
        kind = jnp.full(where_to.shape, KINDS, jnp.int32)
        local = where_to - firsts[KINDS]
        for k in range(KINDS):
            inside = (where_to >= firsts[k]) & (where_to < firsts[k] + owned)
            kind = jnp.where(inside, k, kind)
            local = jnp.where(inside, where_to - firsts[k], local)
        return kind, local

    kind, local = kinds_of(column)
    before = (kind == kinds_of(row)[0]) & (across < down)
    rank = jnp.where(before, 1, 0).sum(1, keepdims=True)
    shape = (groups, 128)
    lane = lax.broadcasted_iota(jnp.int32, shape, 1)
    group = lax.broadcasted_iota(jnp.int32, shape, 0)
    chosen = jnp.where(kind * CAP + rank == lane, group, 0).max(0, keepdims=True)
    here = local == lane
    own = jnp.where(here & (kind == KINDS), group, groups).min(0, keepdims=True)
    slots = [
        jnp.where(here & (kind == k), jnp.minimum(rank, CAP), CAP).min(0, keepdims=True)
        for k in range(KINDS)
    ]
    return jnp.concatenate([chosen, own, *slots, chosen, chosen], axis=0)


def turned(row, length):
    shape = (length, row.shape[1])
    down = lax.broadcasted_iota(jnp.int32, shape, 0)
    across = lax.broadcasted_iota(jnp.int32, shape, 1)
    column = jnp.where(down == across, row, 0).sum(1, keepdims=True)
    return jnp.broadcast_to(column, shape)


def exchange_kernel(sectors, target_hbm, source_hbm, w_hbm, f_hbm, area_hbm, *rest):
    total, received_late, pool, late = rest[:4]
    (target, mine, theirs, source, table, slots, area, wbuf, fbuf, sbuf, received), rest = rest[4:15], rest[15:]
    i_sem, t_sem, f_sem, w_sem, send_sem, recv_sem, tsend_sem, trecv_sem = rest
    me = lax.axis_index("sector")
    owned, width, cols = total.shape
    groups = target.shape[0]
    nb = w_hbm.shape[0]
    per_group = nb // groups
    blocks = f_hbm.shape[0]
    places = [lax.rem(me + sectors + move, sectors) for move in offsets(me)]
    peers = [{"sector": place} for place in places]
    barrier = pltpu.get_barrier_semaphore()
    for peer in peers:
        pl.semaphore_signal(barrier, inc=1, device_id=peer, device_id_type=MESH)

    target_in = pltpu.make_async_copy(target_hbm, target, i_sem.at[0])
    source_in = pltpu.make_async_copy(source_hbm, source, i_sem.at[1])
    target_in.start()
    source_in.start()
    loads = [source_in]
    for ref, buf, sem, size in ((f_hbm, fbuf, f_sem, blocks), (w_hbm, wbuf, w_sem, nb)):
        parts = sem.shape[0]
        for i in range(parts):
            rows = pl.ds(i * (size // parts), size // parts)
            loads.append(pltpu.make_async_copy(ref.at[rows], buf.at[rows], sem.at[i]))
            loads[-1].start()
    area_in = pltpu.make_async_copy(area_hbm, area, i_sem.at[3])
    area_in.start()
    nothing = jnp.zeros((width, cols), jnp.bfloat16)
    fbuf[blocks] = nothing
    for k in range(len(EARLY)):
        received[k * SLOTS + CAP] = nothing
    for k in range(len(LATE)):
        received_late[k * SLOTS + CAP] = nothing

    target_in.wait()
    firsts = [place * owned for place in places] + [me * owned]
    mine[...] = tables(target[...], owned, firsts)
    table_in = pltpu.make_async_copy(mine, table, i_sem.at[2])
    table_in.start()
    pl.semaphore_wait(barrier, KINDS)
    moved = []
    for k in range(KINDS):
        moved.append(
            pltpu.make_async_remote_copy(
                src_ref=mine,
                dst_ref=theirs.at[k],
                send_sem=tsend_sem.at[k],
                recv_sem=trecv_sem.at[k],
                device_id=peers[k],
                device_id_type=MESH,
            )
        )
        moved[-1].start()

    n9 = width // 4
    rows = pool.shape[1]
    row = lax.broadcasted_iota(jnp.int32, (rows, width), 0)
    pixel = lax.broadcasted_iota(jnp.int32, (rows, width), 1)
    member = jnp.where(row < n9, pixel // 4 - row, pixel // 16 - (row - n9)) == 0

    table_in.wait()
    for copy in loads:
        copy.wait()

    def product(g, absent=False):
        first = g * per_group
        left = jnp.concatenate([wbuf[first + q] for q in range(per_group)], axis=1)
        places = [jnp.where(absent, blocks, source[first + q]) for q in range(per_group)]
        right = jnp.concatenate([fbuf[place] for place in places], axis=0)
        return jnp.dot(left, right, preferred_element_type=jnp.float32)

    messages = []
    for i, (k, first, count) in enumerate(SCHEDULE):
        landing = received if k in EARLY else received_late
        start = (EARLY if k in EARLY else LATE).index(k) * SLOTS

        unroll = count if count == UNROLL else count // 2

        @pl.loop(0, count // unroll)
        def _(c):
            for r in range(unroll):
                slot = k * CAP + first + c * unroll + r
                sbuf[slot] = product(table[0, slot]).astype(jnp.bfloat16)

        message = pltpu.make_async_remote_copy(
            src_ref=sbuf.at[pl.ds(k * CAP + first, count)],
            dst_ref=landing.at[pl.ds(start + first, count)],
            send_sem=send_sem.at[i],
            recv_sem=recv_sem.at[i],
            device_id=peers[k],
            device_id_type=MESH,
        )
        message.start()
        messages.append((k, message))

    for copy in moved:
        copy.wait()
    slots_in = [pltpu.make_async_copy(theirs.at[k], slots.at[k], t_sem.at[k]) for k in range(KINDS)]
    for copy in slots_in:
        copy.start()
    for i, k in enumerate(LATE):
        late[i] = turned(theirs[k, 2 + k : 3 + k, :], owned)

    @pl.loop(0, owned // 2)
    def _(i):
        for j in range(2):
            g = table[1, 2 * i + j]
            total[2 * i + j] = product(jnp.minimum(g, groups - 1), g == groups)

    area_in.wait()

    @pl.loop(0, owned)
    def _(t):
        share = jnp.where(member, area[pl.ds(t, 1), :], 0.0)
        pool[t] = (share / share.sum(1, keepdims=True)).astype(pool.dtype)

    for copy in slots_in:
        copy.wait()
    for k, message in messages:
        if k in EARLY:
            message.wait()

    @pl.loop(0, owned // 2)
    def _(i):
        for j in range(2):
            t = 2 * i + j
            value = total[t]
            for e, k in enumerate(EARLY):
                value = value + received[e * SLOTS + slots[k, 2 + k, t]].astype(jnp.float32)
            total[t] = value

    for k, message in messages:
        if k in LATE:
            message.wait()


def exchange(fields, weights, source_block, target_block, area, sectors):
    nb, width, _ = weights.shape
    cols = fields.shape[-1]
    groups = target_block.shape[0]
    owned = area.shape[0]
    blocks = fields.shape[0]
    block = (width, cols)
    bf16, i32 = jnp.bfloat16, jnp.int32
    operands = (target_block, source_block, weights, fields, area)
    return pl.pallas_call(
        functools.partial(exchange_kernel, sectors),
        out_shape=[
            jax.ShapeDtypeStruct((owned, *block), jnp.float32),
            jax.ShapeDtypeStruct((len(LATE) * SLOTS, *block), bf16),
            jax.ShapeDtypeStruct((owned, width // 4 + width // 16, width), bf16),
            jax.ShapeDtypeStruct((len(LATE), owned, 128), i32),
        ],
        in_specs=[HBM] * 5,
        out_specs=[VMEM] * 4,
        scratch_shapes=[
            pltpu.VMEM((groups,), i32),
            pltpu.VMEM((8, 128), i32),
            pltpu.VMEM((KINDS, 8, 128), i32),
            pltpu.SMEM((nb,), i32),
            pltpu.SMEM((8, 128), i32),
            pltpu.SMEM((KINDS, 8, 128), i32),
            pltpu.VMEM(area.shape, jnp.float32),
            pltpu.VMEM(weights.shape, bf16),
            pltpu.VMEM((blocks + 1, *block), bf16),
            pltpu.VMEM((KINDS * CAP, *block), bf16),
            pltpu.VMEM((len(EARLY) * SLOTS, *block), bf16),
        ]
        + [
            pltpu.SemaphoreType.DMA((4,)),
            pltpu.SemaphoreType.DMA((KINDS,)),
            pltpu.SemaphoreType.DMA((FIELD_PARTS,)),
            pltpu.SemaphoreType.DMA((WEIGHT_PARTS,)),
            pltpu.SemaphoreType.DMA((len(SCHEDULE),)),
            pltpu.SemaphoreType.DMA((len(SCHEDULE),)),
            pltpu.SemaphoreType.DMA((KINDS,)),
            pltpu.SemaphoreType.DMA((KINDS,)),
        ],
        compiler_params=pltpu.CompilerParams(
            collective_id=0, has_side_effects=True, vmem_limit_bytes=32 * 2**20
        ),
        name="exchange",
    )(*(pltpu.with_memory_space_constraint(x, pltpu.HBM) for x in operands))


def finish_kernel(total, received, pool, late, *rest):
    outs_hbm, outs, out_sem = rest[:3], rest[3:6], rest[6]
    ten, nine, eight = outs
    owned = total.shape[0]
    n9 = nine.shape[1]

    def results(c):
        rows = pl.ds(c * STEP, STEP)
        return [
            pltpu.make_async_copy(outs[i].at[rows], outs_hbm[i].at[rows], out_sem.at[3 * c + i])
            for i in range(3)
        ]

    for c in range(owned // STEP):
        places = [late[i, pl.ds(c * STEP, STEP), :] for i in range(len(LATE))]
        for j in range(STEP):
            t = c * STEP + j
            value = total[t]
            for i in range(len(LATE)):
                value = value + received[i * SLOTS + places[i][j, 0]].astype(jnp.float32)
            rounded = value.astype(jnp.bfloat16)
            ten[t] = rounded
            means = jnp.dot(pool[t], rounded, preferred_element_type=jnp.float32)
            nine[t] = means[:n9]
            eight[t] = means[n9:]
        for copy in results(c):
            copy.start()

    @pl.loop(0, owned // STEP)
    def _(c):
        for copy in results(c):
            copy.wait()


def finish(total, received, pool, late):
    owned, width, cols = total.shape
    outs = [
        jax.ShapeDtypeStruct((owned, width, cols), jnp.bfloat16),
        jax.ShapeDtypeStruct((owned, width // 4, cols), jnp.float32),
        jax.ShapeDtypeStruct((owned, width // 16, cols), jnp.float32),
    ]
    return pl.pallas_call(
        finish_kernel,
        out_shape=outs,
        in_specs=[VMEM] * 4,
        out_specs=[HBM] * 3,
        scratch_shapes=[pltpu.VMEM(out.shape, out.dtype) for out in outs]
        + [
            pltpu.SemaphoreType.DMA((3 * (owned // STEP),)),
        ],
        compiler_params=pltpu.CompilerParams(vmem_limit_bytes=16 * 2**20),
        name="finish",
    )(total, received, pool, late)


def per_device(fields, weights, source_block, target_block, area):
    width = weights.shape[1]
    cols = fields.shape[1]
    owned = area.shape[0] // width
    sectors = lax.axis_size("sector")
    blocks = fields.reshape(-1, width, cols)
    parts = exchange(
        blocks, weights, source_block, target_block, area.reshape(owned, width), sectors
    )
    ten, nine, eight = finish(*parts)
    return ten.reshape(-1, cols), nine.reshape(-1, cols), eight.reshape(-1, cols)


def solution(mesh):
    in_specs = (
        P(("groups", "sector"), None),
        P("sector", None, None),
        P("sector"),
        P("sector"),
        P("sector"),
    )
    out_specs = (P(("groups", "sector"), None),) * 3
    return jax.shard_map(
        per_device, mesh=mesh, in_specs=in_specs, out_specs=out_specs, check_vma=False
    )
```

```python
import functools

import jax
import jax.numpy as jnp
from jax import lax
from jax.experimental import pallas as pl
from jax.experimental.pallas import tpu as pltpu
from jax.sharding import PartitionSpec as P

CAP = 16
KINDS = 4
SCHEDULE = ((0, 0, 4), (0, 4, 12), (1, 0, 16), (2, 0, 16), (3, 0, 16))
UNROLL = 4
EARLY = (0, 1, 3)
LATE = (2,)
SLOTS = CAP + 1
STEP = 16
FIELD_PARTS = 2
WEIGHT_PARTS = 4
ANY = pl.BlockSpec(memory_space=pl.ANY)
HBM = pl.BlockSpec(memory_space=pltpu.HBM)
VMEM = pl.BlockSpec(memory_space=pltpu.VMEM)
MESH = pl.DeviceIdType.MESH


def offsets(me):
    near = jnp.where(lax.rem(me // 2, 2) == 0, 2, -2)
    here = jnp.where(lax.rem(me, 2) == 0, 1, -1)
    return [near, -near, -here, here]


def tables(target, owned, firsts):
    groups = target.shape[0]
    row = target.reshape(1, groups)
    down = lax.broadcasted_iota(jnp.int32, (groups, groups), 0)
    across = lax.broadcasted_iota(jnp.int32, (groups, groups), 1)
    column = jnp.where(down == across, row, 0).sum(1, keepdims=True)

    def kinds_of(where_to):
        kind = jnp.full(where_to.shape, KINDS, jnp.int32)
        local = where_to - firsts[KINDS]
        for k in range(KINDS):
            inside = (where_to >= firsts[k]) & (where_to < firsts[k] + owned)
            kind = jnp.where(inside, k, kind)
            local = jnp.where(inside, where_to - firsts[k], local)
        return kind, local

    kind, local = kinds_of(column)
    before = (kind == kinds_of(row)[0]) & (across < down)
    rank = jnp.where(before, 1, 0).sum(1, keepdims=True)
    shape = (groups, 128)
    lane = lax.broadcasted_iota(jnp.int32, shape, 1)
    group = lax.broadcasted_iota(jnp.int32, shape, 0)
    chosen = jnp.where(kind * CAP + rank == lane, group, 0).max(0, keepdims=True)
    here = local == lane
    own = jnp.where(here & (kind == KINDS), group, groups).min(0, keepdims=True)
    slots = [
        jnp.where(here & (kind == k), jnp.minimum(rank, CAP), CAP).min(0, keepdims=True)
        for k in range(KINDS)
    ]
    return jnp.concatenate([chosen, own, *slots, chosen, chosen], axis=0)


def turned(row, length):
    shape = (length, row.shape[1])
    down = lax.broadcasted_iota(jnp.int32, shape, 0)
    across = lax.broadcasted_iota(jnp.int32, shape, 1)
    column = jnp.where(down == across, row, 0).sum(1, keepdims=True)
    return jnp.broadcast_to(column, shape)


def exchange_kernel(sectors, target_hbm, source_hbm, w_hbm, f_hbm, area_hbm, *rest):
    total, received_late, pool, late = rest[:4]
    (target, mine, theirs, source, table, slots, area, wbuf, fbuf, sbuf, received), rest = rest[4:15], rest[15:]
    i_sem, t_sem, f_sem, w_sem, send_sem, recv_sem, tsend_sem, trecv_sem = rest
    me = lax.axis_index("sector")
    owned, width, cols = total.shape
    groups = target.shape[0]
    nb = w_hbm.shape[0]
    per_group = nb // groups
    blocks = f_hbm.shape[0]
    places = [lax.rem(me + sectors + move, sectors) for move in offsets(me)]
    peers = [{"sector": place} for place in places]
    barrier = pltpu.get_barrier_semaphore()
    for peer in peers:
        pl.semaphore_signal(barrier, inc=1, device_id=peer, device_id_type=MESH)

    target_in = pltpu.make_async_copy(target_hbm, target, i_sem.at[0])
    source_in = pltpu.make_async_copy(source_hbm, source, i_sem.at[1])
    target_in.start()
    source_in.start()
    loads = [source_in]
    for ref, buf, sem, size in ((f_hbm, fbuf, f_sem, blocks), (w_hbm, wbuf, w_sem, nb)):
        parts = sem.shape[0]
        for i in range(parts):
            rows = pl.ds(i * (size // parts), size // parts)
            loads.append(pltpu.make_async_copy(ref.at[rows], buf.at[rows], sem.at[i]))
            loads[-1].start()
    area_in = pltpu.make_async_copy(area_hbm, area, i_sem.at[3])
    area_in.start()
    nothing = jnp.zeros((width, cols), jnp.bfloat16)
    fbuf[blocks] = nothing
    for k in range(len(EARLY)):
        received[k * SLOTS + CAP] = nothing
    for k in range(len(LATE)):
        received_late[k * SLOTS + CAP] = nothing

    target_in.wait()
    firsts = [place * owned for place in places] + [me * owned]
    mine[...] = tables(target[...], owned, firsts)
    table_in = pltpu.make_async_copy(mine, table, i_sem.at[2])
    table_in.start()
    pl.semaphore_wait(barrier, KINDS)
    moved = []
    for k in range(KINDS):
        moved.append(
            pltpu.make_async_remote_copy(
                src_ref=mine,
                dst_ref=theirs.at[k],
                send_sem=tsend_sem.at[k],
                recv_sem=trecv_sem.at[k],
                device_id=peers[k],
                device_id_type=MESH,
            )
        )
        moved[-1].start()

    n9 = width // 4
    rows = pool.shape[1]
    row = lax.broadcasted_iota(jnp.int32, (rows, width), 0)
    pixel = lax.broadcasted_iota(jnp.int32, (rows, width), 1)
    member = jnp.where(row < n9, pixel // 4 - row, pixel // 16 - (row - n9)) == 0

    table_in.wait()
    for copy in loads:
        copy.wait()

    def product(g, absent=False):
        first = g * per_group
        left = jnp.concatenate([wbuf[first + q] for q in range(per_group)], axis=1)
        places = [jnp.where(absent, blocks, source[first + q]) for q in range(per_group)]
        right = jnp.concatenate([fbuf[place] for place in places], axis=0)
        return jnp.dot(left, right, preferred_element_type=jnp.float32)

    messages = []
    for i, (k, first, count) in enumerate(SCHEDULE):
        landing = received if k in EARLY else received_late
        start = (EARLY if k in EARLY else LATE).index(k) * SLOTS

        @pl.loop(0, count // UNROLL)
        def _(c):
            for r in range(UNROLL):
                slot = k * CAP + first + c * UNROLL + r
                sbuf[slot] = product(table[0, slot]).astype(jnp.bfloat16)

        message = pltpu.make_async_remote_copy(
            src_ref=sbuf.at[pl.ds(k * CAP + first, count)],
            dst_ref=landing.at[pl.ds(start + first, count)],
            send_sem=send_sem.at[i],
            recv_sem=recv_sem.at[i],
            device_id=peers[k],
            device_id_type=MESH,
        )
        message.start()
        messages.append((k, message))

    for copy in moved:
        copy.wait()
    slots_in = [pltpu.make_async_copy(theirs.at[k], slots.at[k], t_sem.at[k]) for k in range(KINDS)]
    for copy in slots_in:
        copy.start()
    for i, k in enumerate(LATE):
        late[i] = turned(theirs[k, 2 + k : 3 + k, :], owned)

    @pl.loop(0, owned // 2)
    def _(i):
        for j in range(2):
            g = table[1, 2 * i + j]
            total[2 * i + j] = product(jnp.minimum(g, groups - 1), g == groups)

    area_in.wait()

    @pl.loop(0, owned)
    def _(t):
        share = jnp.where(member, area[pl.ds(t, 1), :], 0.0)
        pool[t] = (share / share.sum(1, keepdims=True)).astype(pool.dtype)

    for copy in slots_in:
        copy.wait()
    for k, message in messages:
        if k in EARLY:
            message.wait()

    @pl.loop(0, owned // 2)
    def _(i):
        for j in range(2):
            t = 2 * i + j
            value = total[t]
            for e, k in enumerate(EARLY):
                value = value + received[e * SLOTS + slots[k, 2 + k, t]].astype(jnp.float32)
            total[t] = value

    for k, message in messages:
        if k in LATE:
            message.wait()


def exchange(fields, weights, source_block, target_block, area, sectors):
    nb, width, _ = weights.shape
    cols = fields.shape[-1]
    groups = target_block.shape[0]
    owned = area.shape[0]
    blocks = fields.shape[0]
    block = (width, cols)
    bf16, i32 = jnp.bfloat16, jnp.int32
    operands = (target_block, source_block, weights, fields, area)
    return pl.pallas_call(
        functools.partial(exchange_kernel, sectors),
        out_shape=[
            jax.ShapeDtypeStruct((owned, *block), jnp.float32),
            jax.ShapeDtypeStruct((len(LATE) * SLOTS, *block), bf16),
            jax.ShapeDtypeStruct((owned, width // 4 + width // 16, width), bf16),
            jax.ShapeDtypeStruct((len(LATE), owned, 128), i32),
        ],
        in_specs=[HBM] * 5,
        out_specs=[VMEM] * 4,
        scratch_shapes=[
            pltpu.VMEM((groups,), i32),
            pltpu.VMEM((8, 128), i32),
            pltpu.VMEM((KINDS, 8, 128), i32),
            pltpu.SMEM((nb,), i32),
            pltpu.SMEM((8, 128), i32),
            pltpu.SMEM((KINDS, 8, 128), i32),
            pltpu.VMEM(area.shape, jnp.float32),
            pltpu.VMEM(weights.shape, bf16),
            pltpu.VMEM((blocks + 1, *block), bf16),
            pltpu.VMEM((KINDS * CAP, *block), bf16),
            pltpu.VMEM((len(EARLY) * SLOTS, *block), bf16),
        ]
        + [
            pltpu.SemaphoreType.DMA((4,)),
            pltpu.SemaphoreType.DMA((KINDS,)),
            pltpu.SemaphoreType.DMA((FIELD_PARTS,)),
            pltpu.SemaphoreType.DMA((WEIGHT_PARTS,)),
            pltpu.SemaphoreType.DMA((len(SCHEDULE),)),
            pltpu.SemaphoreType.DMA((len(SCHEDULE),)),
            pltpu.SemaphoreType.DMA((KINDS,)),
            pltpu.SemaphoreType.DMA((KINDS,)),
        ],
        compiler_params=pltpu.CompilerParams(
            collective_id=0, has_side_effects=True, vmem_limit_bytes=32 * 2**20
        ),
        name="exchange",
    )(*(pltpu.with_memory_space_constraint(x, pltpu.HBM) for x in operands))


def finish_kernel(total, received, pool, late, *rest):
    outs_hbm, outs, out_sem = rest[:3], rest[3:6], rest[6]
    ten, nine, eight = outs
    owned = total.shape[0]
    n9 = nine.shape[1]

    def results(c):
        rows = pl.ds(c * STEP, STEP)
        return [
            pltpu.make_async_copy(outs[i].at[rows], outs_hbm[i].at[rows], out_sem.at[3 * c + i])
            for i in range(3)
        ]

    for c in range(owned // STEP):
        places = [late[i, pl.ds(c * STEP, STEP), :] for i in range(len(LATE))]
        for j in range(STEP):
            t = c * STEP + j
            value = total[t]
            for i in range(len(LATE)):
                value = value + received[i * SLOTS + places[i][j, 0]].astype(jnp.float32)
            rounded = value.astype(jnp.bfloat16)
            ten[t] = rounded
            means = jnp.dot(pool[t], rounded, preferred_element_type=jnp.float32)
            nine[t] = means[:n9]
            eight[t] = means[n9:]
        for copy in results(c):
            copy.start()

    @pl.loop(0, owned // STEP)
    def _(c):
        for copy in results(c):
            copy.wait()


def finish(total, received, pool, late):
    owned, width, cols = total.shape
    outs = [
        jax.ShapeDtypeStruct((owned, width, cols), jnp.bfloat16),
        jax.ShapeDtypeStruct((owned, width // 4, cols), jnp.float32),
        jax.ShapeDtypeStruct((owned, width // 16, cols), jnp.float32),
    ]
    return pl.pallas_call(
        finish_kernel,
        out_shape=outs,
        in_specs=[VMEM] * 4,
        out_specs=[HBM] * 3,
        scratch_shapes=[pltpu.VMEM(out.shape, out.dtype) for out in outs]
        + [
            pltpu.SemaphoreType.DMA((3 * (owned // STEP),)),
        ],
        compiler_params=pltpu.CompilerParams(vmem_limit_bytes=16 * 2**20),
        name="finish",
    )(total, received, pool, late)


def per_device(fields, weights, source_block, target_block, area):
    width = weights.shape[1]
    cols = fields.shape[1]
    owned = area.shape[0] // width
    sectors = lax.axis_size("sector")
    blocks = fields.reshape(-1, width, cols)
    parts = exchange(
        blocks, weights, source_block, target_block, area.reshape(owned, width), sectors
    )
    ten, nine, eight = finish(*parts)
    return ten.reshape(-1, cols), nine.reshape(-1, cols), eight.reshape(-1, cols)


def solution(mesh):
    in_specs = (
        P(("groups", "sector"), None),
        P("sector", None, None),
        P("sector"),
        P("sector"),
        P("sector"),
    )
    out_specs = (P(("groups", "sector"), None),) * 3
    return jax.shard_map(
        per_device, mesh=mesh, in_specs=in_specs, out_specs=out_specs, check_vma=False
    )
```
